256 devices in a mesh: pair: 8 (over y, x_hi), mode: 32 (over z, x_lo, core).
Axes of the slice: x: 4 (x_hi: 2, x_lo: 2; x = x_hi * 2 + x_lo), y: 4, z: 8, core: 2. Of those that a mesh axis runs over, the one named last changes fastest.
Arguments:
- phi: bfloat16 [8, 384, 384, 384], P('pair', 'mode'), may hold values from -6 to 6
- eigvecs: bfloat16 [12, 384, 384], replicated, may hold values from -0.3125 to 0.3125
- freqs: float32 [12, 384], replicated, may hold values from 0.5 to 8
- occupations: float32 [12, 384], replicated, may hold values from 0.02 to 4
- smearing: float32 [12, 384], replicated, may hold values from 0.2 to 1
- probes: float32 [8, 2], P('pair'), may hold values from 0.5 to 8
- pair_index: int32 [8, 3], P('pair'), may hold values from 0 to 11
Outputs:
- sigma: float32 [384, 2, 384], P('mode', None, 'pair')
The draws below stay inside these ranges and needn't reach their ends.
All inputs are finite; a program needn't handle non-finite values.
Results may differ from the reference program's by a relative error of at most 0.0013.
Values may be sent and summed in bfloat16 or wider, within the bound.
A program may use at most 64 MiB of HBM per device.

```python
import math
import jax
import jax.numpy as jnp
from jax import lax

M = 384
Q = 12
PAIRS = 8


def place_ends(values, key, least, high):
    longest = values.shape.index(max(values.shape))
    spots = []
    for shift in (0, 1):
        where = [jax.random.randint(jax.random.fold_in(key, axis), (), 0, length) for axis, length in enumerate(values.shape)]
        where[longest] = (where[longest] + shift) % values.shape[longest]
        spots.append(tuple(where))
    return values.at[spots[0]].set(least).at[spots[1]].set(high)


def shard_levels(rng, shape, cuts, least, high):
    def one(dim, parts):
        heights = jax.random.uniform(jax.random.fold_in(jax.random.fold_in(rng, 6), dim), (parts,), jnp.float32, least / len(cuts), high / len(cuts))
        return jnp.repeat(jnp.exp(heights), shape[dim] // parts).reshape((-1,) + (1,) * (len(shape) - dim - 1))

    gain = one(*cuts[0])
    for cut in cuts[1:]:
        gain = gain * one(*cut)
    return gain


def scatter_about(rng, extent, scale, most, split=(), held_as=jnp.bfloat16):
    array = jax.random.normal(rng, extent, jnp.float32) * scale
    if len(split) > 0:
        array = shard_levels(rng, extent, split, -0.22, 0.18) * array
    return jnp.clip(array, min=-most, max=most).astype(held_as)


def setup_inputs(seed: int = 0) -> dict:
    key_list = jax.random.split(jax.random.key(seed), 8)
    phi = scatter_about(key_list[0], (PAIRS, M, M, M), 1.0, 6.0, ((0, 8), (1, 32)))
    eigvecs = scatter_about(key_list[1], (Q, M, M), M ** -0.5, 0.3125)
    freqs = jnp.clip(jnp.exp(jax.random.uniform(key_list[2], (Q, M), jnp.float32, math.log(0.5), math.log(8.0))), 0.5, 8.0)
    occupations = jnp.clip(jnp.exp(jax.random.uniform(key_list[3], (Q, M), jnp.float32, math.log(0.02), math.log(4.0))), 0.02, 4.0)
    smearing = jnp.clip(jnp.exp(jax.random.uniform(key_list[4], (Q, M), jnp.float32, math.log(0.2), math.log(1.0))), 0.2, 1.0)
    probes = jnp.clip(0.5 + 7.5 * jax.random.uniform(key_list[5], (PAIRS, 2), jnp.float32) ** shard_levels(key_list[5], (PAIRS, 2), ((0, 8),), -0.2, 0.2), 0.5, 8.0)
    pair_index = place_ends(jax.random.randint(key_list[6], (PAIRS, 3), 0, Q), jax.random.fold_in(key_list[6], 1), 0, Q - 1).astype(jnp.int32)
    return dict(phi=phi, eigvecs=eigvecs, freqs=freqs, occupations=occupations, smearing=smearing, probes=probes, pair_index=pair_index)


def lorentz(offset, eta):
    return eta / (offset * offset + eta * eta)

def weights(f_one, n_one, h_one, f_two, n_two, h_two, omegas):
    total = f_two[:, None] + f_one[None, :]
    differ = f_two[:, None] - f_one[None, :]
    eta = 0.5 * (h_two[:, None] + h_one[None, :])
    bose_sum = 1.0 + n_one[None, :] + n_two[:, None]
    bose_diff = n_one[None, :] - n_two[:, None]
    result = []
    for probe in range(2):
        omega = omegas[probe]
        value = bose_sum * (lorentz(omega - total, eta) - lorentz(omega + total, eta))
        value = value + bose_diff * (lorentz(omega - differ, eta) - lorentz(omega + differ, eta))
        result.append(value)
    return jnp.stack(result)

def reference(phi, eigvecs, freqs, occupations, smearing, probes, pair_index):
    gram = jnp.zeros((M, 2, M), jnp.float32)
    for pidx in range(PAIRS):
        q_one = pair_index[pidx, 0]
        q_two = pair_index[pidx, 1]
        q_three = pair_index[pidx, 2]
        e_one = eigvecs[q_one]
        e_two = eigvecs[q_two]
        e_three = eigvecs[q_three]
        first = jnp.dot(phi[pidx].reshape(M * M, M), e_one, preferred_element_type=jnp.float32)
        first = first.astype(jnp.bfloat16).reshape(M, M, M)
        second = jnp.einsum('cbi,bj->cji', first.astype(jnp.float32), e_two.astype(jnp.float32))
        second = second.astype(jnp.bfloat16)
        rotated = lax.dot_general(e_three, second.reshape(M, M * M), (((0,), (0,)), ((), ())), preferred_element_type=jnp.float32).astype(jnp.bfloat16)
        wgt = weights(freqs[q_one], occupations[q_one], smearing[q_one], freqs[q_two], occupations[q_two], smearing[q_two], probes[pidx])
        for probe in range(2):
            weighted = (wgt[probe].reshape(1, M * M) * rotated.astype(jnp.float32)).astype(jnp.bfloat16)
            part = lax.dot_general(weighted, rotated, (((1,), (1,)), ((), ())), preferred_element_type=jnp.float32)
            gram = gram.at[:, probe, :].add(part)
    offdiag = (jnp.arange(M)[:, None] != jnp.arange(M)[None, :]).astype(jnp.float32)
    scale = 1.0 / (M * math.sqrt(PAIRS))
    return gram * offdiag[:, None, :] * scale
```

```python
import math

import jax
import jax.numpy as jnp
import numpy as np
from jax import lax
from jax.experimental import pallas as pl
from jax.experimental.pallas import tpu as pltpu
from jax.sharding import PartitionSpec as P

MESH = pl.DeviceIdType.MESH
F32 = jnp.float32
BF16 = jnp.bfloat16

M = 384
Z = 8
G = 4
L = 128
NB = M // L
B = M // (Z * G)
ROWS = B * B
PEERS = Z * G - 1
PAIRS = 8
PLANE = 15


def lorentz(offset, eta):
    return eta / (offset * offset + eta * eta)


def dot(a, b, dims=((1,), (0,))):
    return lax.dot_general(a, b, (dims, ((), ())), preferred_element_type=F32)


def kernel(
    pidx, probes, phi, eig, freqs, occ, smear, perm, out,
    e_two_t, e_one, e_three_t, u_f, u_b, send, recv, wgt, acc, half_own, half_got, plane_src,
    plane_got, turned, z_got,
    a_send, a_recv, c_send, c_recv, p_send, p_recv, z_send, z_recv, local,
):
    mode = lax.axis_index("mode")
    pair = lax.axis_index("pair")
    z = mode // G
    g = lax.rem(mode, G)
    xl = g // 2
    core = lax.rem(g, 2)
    y = pair // 2
    xh = lax.rem(pair, 2)

    def mate(e):
        return lax.rem(xl + e // 2, 2) * 2 + lax.rem(core + e % 2, 2)

    def plane_peer(d):
        return lax.rem(y + d // 4, 4), lax.rem(xh + (d // 2) % 2, 2), lax.rem(xl + d % 2, 2)

    def plane_back(d):
        return lax.rem(y + 4 - d // 4, 4), lax.rem(xh + (d // 2) % 2, 2), lax.rem(xl + d % 2, 2)

    barrier = pltpu.get_barrier_semaphore()

    def greet(i, carry):
        other = lax.rem(mode + 1 + i, Z * G)
        pl.semaphore_signal(barrier, inc=1, device_id=(pair, other), device_id_type=MESH)
        return carry

    lax.fori_loop(0, PEERS, greet, 0)
    for d in range(2, PLANE + 1):
        yy, hh, ll = plane_back(d)
        pl.semaphore_signal(
            barrier, inc=1, device_id=(yy * 2 + hh, z * G + ll * 2 + core), device_id_type=MESH
        )

    q_one = pidx[0, 0]
    q_two = pidx[0, 1]
    q_three = pidx[0, 2]
    rows_i = lax.broadcasted_iota(jnp.int32, (M, M), 0)
    cols_i = lax.broadcasted_iota(jnp.int32, (M, M), 1)
    eye = (rows_i == cols_i).astype(F32).astype(BF16)
    e_two_t[...] = dot(eye, eig[q_two], ((1,), (1,))).astype(BF16)
    e_three_t[...] = dot(perm[...], eig[q_three], ((1,), (1,))).astype(BF16)
    e_one[...] = eig[q_one]

    def rotate_two(c, carry):
        rows = dot(e_two_t[...], phi[0, c])
        for b in range(NB):
            u_f[b, pl.ds(c, M, stride=B), :] = rows[:, b * L : (b + 1) * L]
        return carry

    lax.fori_loop(0, B, rotate_two, 0)

    def ship(chunk, peer, zz, gg):
        return pltpu.make_async_remote_copy(
            src_ref=send.at[chunk, zz * G + gg],
            dst_ref=recv.at[chunk, :, pl.ds(3 * mode, 3)],
            send_sem=a_send.at[chunk, peer],
            recv_sem=a_recv.at[chunk, peer],
            device_id=(pair, zz * G + gg),
            device_id_type=MESH,
        )

    def keep(chunk):
        return pltpu.make_async_copy(
            send.at[chunk, mode], recv.at[chunk, :, pl.ds(3 * mode, 3)], local.at[chunk]
        )

    def far(t):
        h = (t + 1) // 2
        return lax.rem(z + 4 + (1 - 2 * lax.rem(t, 2)) * h, Z)

    def first_chunk(zz):
        start = pl.multiple_of(zz * (G * ROWS), G * ROWS)
        rows = jnp.concatenate(
            [u_f[b, pl.ds(start, G * ROWS), :] for b in range(NB)], axis=1
        ).astype(BF16)
        u_b[pl.ds(start, G * ROWS), :] = rows
        done = dot(rows, e_one[:, :L]).astype(BF16)
        send.at[0, pl.ds(zz * G, G)].reshape(G * ROWS, L)[...] = done

    def later_chunks(zz):
        start = pl.multiple_of(zz * (G * ROWS), G * ROWS)
        done = dot(u_b[pl.ds(start, G * ROWS), :], e_one[:, L:]).astype(BF16)
        for chunk in range(1, NB):
            send.at[chunk, pl.ds(zz * G, G)].reshape(G * ROWS, L)[...] = done[
                :, (chunk - 1) * L : chunk * L
            ]

    def ship_all(chunk, t):
        zz = far(t)
        for e in range(G):
            ship(chunk, t * G + e, zz, mate(e)).start()

    def ship_near(chunk):
        for e in range(1, G):
            ship(chunk, (Z - 1) * G + e - 1, z, mate(e)).start()
        keep(chunk).start()

    first_chunk(far(0))
    pl.semaphore_wait(barrier, PEERS + PLANE - 1)
    ship_all(0, 0)

    def step_first(t, carry):
        first_chunk(far(t))
        ship_all(0, t)
        return carry

    lax.fori_loop(1, Z - 1, step_first, 0)
    first_chunk(z)
    ship_near(0)

    def step_later(t, carry):
        later_chunks(far(t))
        ship_all(1, t)
        return carry

    lax.fori_loop(0, Z - 1, step_later, 0)
    later_chunks(z)
    ship_near(1)

    def step_last(t, carry):
        ship_all(2, t)
        return carry

    lax.fori_loop(0, Z - 1, step_last, 0)
    ship_near(2)

    lane = lax.broadcasted_iota(jnp.int32, (B, M), 1)
    mine = lane == mode * B + lax.broadcasted_iota(jnp.int32, (B, M), 0)

    def column(table):
        return jnp.sum(jnp.where(mine, table[pl.ds(q_two, 1), :], 0.0), axis=1, keepdims=True)

    f_one = freqs[pl.ds(q_one, 1), :]
    n_one = occ[pl.ds(q_one, 1), :]
    h_one = smear[pl.ds(q_one, 1), :]
    f_two = column(freqs)
    n_two = column(occ)
    h_two = column(smear)
    total = f_two + f_one
    differ = f_two - f_one
    eta = 0.5 * (h_two + h_one)
    bose_sum = 1.0 + n_one + n_two
    bose_diff = n_one - n_two
    for w in range(2):
        omega = probes[0, w]
        value = bose_sum * (lorentz(omega - total, eta) - lorentz(omega + total, eta))
        value = value + bose_diff * (lorentz(omega - differ, eta) - lorentz(omega + differ, eta))
        for j in range(B):
            wgt[w, j] = value[j : j + 1, :]

    acc[...] = jnp.zeros_like(acc)
    span = M // G

    def take(chunk):
        def wait_one(i, carry):
            ship(chunk, i, z, mate(1)).wait_recv()
            return carry

        lax.fori_loop(0, PEERS, wait_one, 0)
        keep(chunk).wait()

        def gram(jp, carry):
            block = jnp.concatenate(
                [recv.at[chunk, 2 * jp + s].reshape(M, L)[...] for s in range(2)], axis=1
            )
            rot = dot(e_three_t[...], block).astype(BF16)
            hole = jnp.zeros((L - span, 2 * L), BF16)
            parts = []
            for k in range(G):
                parts += [rot[k * span : (k + 1) * span], hole]
            right = jnp.concatenate(parts, axis=0)
            wide = rot.astype(F32)
            for w in range(2):
                row = jnp.concatenate(
                    [wgt[w, 2 * jp + s, :, chunk * L : (chunk + 1) * L] for s in range(2)],
                    axis=1,
                )
                part = dot((wide * row).astype(BF16), right, ((1,), (1,)))
                for k in range(G):
                    acc[k, w * M : (w + 1) * M, :] += part[:, k * L : (k + 1) * L]
            return carry

        lax.fori_loop(0, B // 2, gram, 0)

    for chunk in range(NB):
        take(chunk)

    for s in range(2):
        half_own.at[s].reshape(2 * M, L)[...] = acc[2 * s + 1 - core].astype(BF16)
    swaps = []
    for s in range(2):
        swap = pltpu.make_async_remote_copy(
            src_ref=half_own.at[s],
            dst_ref=half_got.at[s],
            send_sem=c_send.at[s],
            recv_sem=c_recv.at[s],
            device_id=(pair, z * G + xl * 2 + 1 - core),
            device_id_type=MESH,
        )
        swap.start()
        swaps.append(swap)
    for s in range(2):
        swaps[s].wait_recv()
        both = acc[2 * s + core] + half_got.at[s].reshape(2 * M, L)[...].astype(F32)
        plane_src.at[s].reshape(2 * M, L)[...] = both.astype(BF16)

    hops = []
    for d in range(1, PLANE + 1):
        yy, hh, ll = plane_peer(d)
        hop = pltpu.make_async_remote_copy(
            src_ref=plane_src.at[ll, :, :, yy * 2 + hh],
            dst_ref=plane_got.at[d],
            send_sem=p_send.at[d - 1],
            recv_sem=p_recv.at[d - 1],
            device_id=(yy * 2 + hh, z * G + ll * 2 + core),
            device_id_type=MESH,
        )
        hop.start()
        hops.append(hop)
    wide_rows = 2 * M // PAIRS
    kept = pltpu.make_async_copy(plane_src.at[xl, :, :, pair], plane_got.at[0], local.at[NB])
    kept.start()
    kept.wait()
    for hop in hops:
        hop.wait_recv()
    whole = plane_got.at[0].reshape(wide_rows, L)[...].astype(F32)
    for d in range(1, PLANE + 1):
        whole = whole + plane_got.at[d].reshape(wide_rows, L)[...].astype(F32)

    square = jnp.concatenate([whole, jnp.zeros((L - wide_rows, L), F32)], axis=0)
    turned.reshape(L, L)[...] = square.T
    rises = []
    for d in range(1, Z):
        zz = lax.rem(z + d, Z)
        rise = pltpu.make_async_remote_copy(
            src_ref=turned.at[pl.ds(3 * zz, 3)],
            dst_ref=z_got.at[d],
            send_sem=z_send.at[d - 1],
            recv_sem=z_recv.at[d - 1],
            device_id=(pair, zz * G + g),
            device_id_type=MESH,
        )
        rise.start()
        rises.append(rise)
    stay = pltpu.make_async_copy(turned.at[pl.ds(3 * z, 3)], z_got.at[0], local.at[NB + 1])
    stay.start()
    stay.wait()
    for rise in rises:
        rise.wait_recv()
    result = z_got.at[0].reshape(B, L)[...]
    for d in range(1, Z):
        result = result + z_got.at[d].reshape(B, L)[...]

    cols = M // PAIRS
    row_id = mode * B + lax.broadcasted_iota(jnp.int32, (B, cols), 0)
    col_id = pair * cols + lax.broadcasted_iota(jnp.int32, (B, cols), 1)
    scale = 1.0 / (M * math.sqrt(PAIRS))
    for w in range(2):
        out[:, w, :] = jnp.where(row_id == col_id, 0.0, result[:, w * cols : (w + 1) * cols] * scale)

    def sent(i, carry):
        for chunk in range(NB):
            ship(chunk, i, z, mate(1)).wait_send()
        return carry

    lax.fori_loop(0, PEERS, sent, 0)
    for copy in swaps + hops + rises:
        copy.wait_send()


def shards(phi, eigvecs, freqs, occupations, smearing, probes, pair_index):
    k = np.arange(M)
    natural = (k % (M // G)) // B * (G * B) + k // (M // G) * B + k % B
    perm = jnp.asarray(np.equal(natural[:, None], k[None, :]), BF16)
    vmem = pl.BlockSpec(memory_space=pltpu.VMEM)
    smem = pl.BlockSpec(memory_space=pltpu.SMEM)
    dma = pltpu.SemaphoreType.DMA
    return pl.pallas_call(
        kernel,
        out_shape=jax.ShapeDtypeStruct((B, 2, M // PAIRS), F32),
        in_specs=[smem, smem] + [vmem] * 6,
        out_specs=vmem,
        scratch_shapes=[
            pltpu.VMEM((M, M), BF16),
            pltpu.VMEM((M, M), BF16),
            pltpu.VMEM((M, M), BF16),
            pltpu.VMEM((NB, M * B, L), F32),
            pltpu.VMEM((M * B, M), BF16),
            pltpu.VMEM((NB, Z * G, B, 3, 4, L), BF16),
            pltpu.VMEM((NB, B, M // 4, 4, L), BF16),
            pltpu.VMEM((2, B, 1, M), F32),
            pltpu.VMEM((G, 2 * M, L), F32),
            pltpu.VMEM((2, 2 * M // 4, 4, L), BF16),
            pltpu.VMEM((2, 2 * M // 4, 4, L), BF16),
            pltpu.VMEM((2, 2, G, Z, 3, 4, L), BF16),
            pltpu.VMEM((PLANE + 1, 2, G, 3, 4, L), BF16),
            pltpu.VMEM((L // 4, 4, L), F32),
            pltpu.VMEM((Z, 3, 4, L), F32),
            dma((NB, PEERS)),
            dma((NB, PEERS)),
            dma((2,)),
            dma((2,)),
            dma((PLANE,)),
            dma((PLANE,)),
            dma((Z - 1,)),
            dma((Z - 1,)),
            dma((NB + 2,)),
        ],
        compiler_params=pltpu.CompilerParams(
            collective_id=0, has_side_effects=True, vmem_limit_bytes=60 * 1024 * 1024
        ),
        name="sigma",
    )(pair_index, probes, phi, eigvecs, freqs, occupations, smearing, perm)


def solution(mesh):
    return jax.shard_map(
        shards,
        mesh=mesh,
        in_specs=(
            P("pair", "mode", None, None),
            P(),
            P(),
            P(),
            P(),
            P("pair", None),
            P("pair", None),
        ),
        out_specs=P("mode", None, "pair"),
        check_vma=False,
    )
```

```python
import math

import jax
import jax.numpy as jnp
import numpy as np
from jax import lax
from jax.experimental import pallas as pl
from jax.experimental.pallas import tpu as pltpu
from jax.sharding import PartitionSpec as P

MESH = pl.DeviceIdType.MESH
F32 = jnp.float32
BF16 = jnp.bfloat16

M = 384
Z = 8
G = 4
L = 128
NB = M // L
B = M // (Z * G)
ROWS = B * B
PEERS = Z * G - 1
PAIRS = 8
PLANE = 15
PIECES = ((0, 0, 12), (1, 0, 12), (2, 0, 6), (2, 6, 4), (2, 10, 2))
NP = len(PIECES)


def lorentz(offset, eta):
    return eta / (offset * offset + eta * eta)


def dot(a, b, dims=((1,), (0,))):
    return lax.dot_general(a, b, (dims, ((), ())), preferred_element_type=F32)


def kernel(
    pidx, probes, phi_hbm, eig_hbm, freqs, occ, smear, perm, out,
    phi, eig, lhs, right_s, e_two_t, e_one, e_three_t, u_f, u_b, send, recv, wgt, acc, half_own, half_got, plane_src,
    plane_got, turned, z_got,
    a_send, a_recv, c_send, c_recv, p_send, p_recv, z_send, z_recv, local, loads,
):
    mode = lax.axis_index("mode")
    pair = lax.axis_index("pair")
    z = mode // G
    g = lax.rem(mode, G)
    xl = g // 2
    core = lax.rem(g, 2)
    y = pair // 2
    xh = lax.rem(pair, 2)

    def mate(e):
        return lax.rem(xl + e // 2, 2) * 2 + lax.rem(core + e % 2, 2)

    def plane_peer(d):
        return lax.rem(y + d // 4, 4), lax.rem(xh + (d // 2) % 2, 2), lax.rem(xl + d % 2, 2)

    def plane_back(d):
        return lax.rem(y + 4 - d // 4, 4), lax.rem(xh + (d // 2) % 2, 2), lax.rem(xl + d % 2, 2)

    load_eig = pltpu.make_async_copy(eig_hbm, eig, loads.at[B // 2])
    load_eig.start()

    def load_phi(n):
        two = pl.ds(2 * n, 2)
        return pltpu.make_async_copy(phi_hbm.at[0, two], phi.at[two], loads.at[n])

    for n in range(B // 2):
        load_phi(n).start()

    barrier = pltpu.get_barrier_semaphore()

    def greet(i, carry):
        other = lax.rem(mode + 1 + i, Z * G)
        pl.semaphore_signal(barrier, inc=1, device_id=(pair, other), device_id_type=MESH)
        return carry

    lax.fori_loop(0, PEERS, greet, 0)
    for d in range(2, PLANE + 1):
        yy, hh, ll = plane_back(d)
        pl.semaphore_signal(
            barrier, inc=1, device_id=(yy * 2 + hh, z * G + ll * 2 + core), device_id_type=MESH
        )

    load_eig.wait()
    q_one = pidx[0, 0]
    q_two = pidx[0, 1]
    q_three = pidx[0, 2]
    rows_i = lax.broadcasted_iota(jnp.int32, (M, M), 0)
    cols_i = lax.broadcasted_iota(jnp.int32, (M, M), 1)
    eye = (rows_i == cols_i).astype(F32).astype(BF16)
    e_two_t[...] = dot(eye, eig[q_two], ((1,), (1,))).astype(BF16)
    e_three_t[...] = dot(perm[...], eig[q_three], ((1,), (1,))).astype(BF16)
    e_one[...] = eig[q_one]

    def rotate_two(n, carry):
        load_phi(n).wait()
        rows = dot(e_two_t[...], jnp.concatenate([phi[2 * n], phi[2 * n + 1]], axis=1))
        for c in range(2):
            for b in range(NB):
                u_f[b, pl.ds(2 * n + c, M, stride=B), :] = rows[
                    :, c * M + b * L : c * M + (b + 1) * L
                ]
        return carry

    lax.fori_loop(0, B // 2, rotate_two, 0)

    def ship(piece, peer, zz, gg):
        chunk, j, nj = PIECES[piece]
        return pltpu.make_async_remote_copy(
            src_ref=send.at[chunk, zz * G + gg, pl.ds(j, nj)],
            dst_ref=recv.at[chunk, pl.ds(j, nj), pl.ds(3 * mode, 3)],
            send_sem=a_send.at[piece, peer],
            recv_sem=a_recv.at[piece, peer],
            device_id=(pair, zz * G + gg),
            device_id_type=MESH,
        )

    def keep(chunk):
        return pltpu.make_async_copy(
            send.at[chunk, mode], recv.at[chunk, :, pl.ds(3 * mode, 3)], local.at[chunk]
        )

    def far(t):
        h = (t + 1) // 2
        return lax.rem(z + 4 + (1 - 2 * lax.rem(t, 2)) * h, Z)

    def first_chunk(zz):
        start = pl.multiple_of(zz * (G * ROWS), G * ROWS)
        rows = jnp.concatenate(
            [u_f[b, pl.ds(start, G * ROWS), :] for b in range(NB)], axis=1
        ).astype(BF16)
        u_b[pl.ds(start, G * ROWS), :] = rows
        done = dot(rows, e_one[:, :L]).astype(BF16)
        send.at[0, pl.ds(zz * G, G)].reshape(G * ROWS, L)[...] = done

    def later_chunks(zz):
        start = pl.multiple_of(zz * (G * ROWS), G * ROWS)
        done = dot(u_b[pl.ds(start, G * ROWS), :], e_one[:, L:]).astype(BF16)
        for chunk in range(1, NB):
            send.at[chunk, pl.ds(zz * G, G)].reshape(G * ROWS, L)[...] = done[
                :, (chunk - 1) * L : chunk * L
            ]

    def ship_all(piece, t):
        zz = far(t)
        for e in range(G):
            ship(piece, t * G + e, zz, mate(e)).start()

    def ship_near(piece):
        for e in range(1, G):
            ship(piece, (Z - 1) * G + e - 1, z, mate(e)).start()

    first_chunk(far(0))
    pl.semaphore_wait(barrier, PEERS + PLANE - 1)
    ship_all(0, 0)

    def step_first(t, carry):
        first_chunk(far(t))
        ship_all(0, t)
        return carry

    lax.fori_loop(1, Z - 1, step_first, 0)
    first_chunk(z)
    ship_near(0)
    keep(0).start()

    def step_later(t, carry):
        later_chunks(far(t))
        ship_all(1, t)
        return carry

    lax.fori_loop(0, Z - 1, step_later, 0)
    later_chunks(z)
    ship_near(1)
    keep(1).start()
    keep(2).start()

    for piece in range(2, NP):

        def step_last(t, carry, piece=piece):
            ship_all(piece, t)
            return carry

        lax.fori_loop(0, Z - 1, step_last, 0)
        ship_near(piece)

    lane = lax.broadcasted_iota(jnp.int32, (B, M), 1)
    mine = lane == mode * B + lax.broadcasted_iota(jnp.int32, (B, M), 0)

    def column(table):
        return jnp.sum(jnp.where(mine, table[pl.ds(q_two, 1), :], 0.0), axis=1, keepdims=True)

    f_one = freqs[pl.ds(q_one, 1), :]
    n_one = occ[pl.ds(q_one, 1), :]
    h_one = smear[pl.ds(q_one, 1), :]
    f_two = column(freqs)
    n_two = column(occ)
    h_two = column(smear)
    total = f_two + f_one
    differ = f_two - f_one
    eta = 0.5 * (h_two + h_one)
    bose_sum = 1.0 + n_one + n_two
    bose_diff = n_one - n_two
    for w in range(2):
        omega = probes[0, w]
        value = bose_sum * (lorentz(omega - total, eta) - lorentz(omega + total, eta))
        value = value + bose_diff * (lorentz(omega - differ, eta) - lorentz(omega + differ, eta))
        for j in range(B):
            wgt[w, j] = value[j : j + 1, :]

    acc[...] = jnp.zeros_like(acc)
    span = M // G

    def rotated(chunk, jp):
        block = jnp.concatenate(
            [recv.at[chunk, 2 * jp + s].reshape(M, L)[...] for s in range(2)], axis=1
        )
        rot = dot(e_three_t[...], block).astype(BF16)
        wide = rot.astype(F32)
        weighted = []
        for w in range(2):
            row = jnp.concatenate(
                [wgt[w, 2 * jp + s, :, chunk * L : (chunk + 1) * L] for s in range(2)], axis=1
            )
            weighted.append((wide * row).astype(BF16))
        return rot, weighted

    hole = jnp.zeros((L - span, 2 * L), BF16)

    def arrive(piece):
        def wait_one(i, carry):
            ship(piece, i, z, mate(1)).wait_recv()
            return carry

        lax.fori_loop(0, PEERS, wait_one, 0)

    def gram(chunk, jp):
        rot, weighted = rotated(chunk, jp)
        parts = []
        for k in range(G):
            parts += [rot[k * span : (k + 1) * span], hole]
        right = jnp.concatenate(parts, axis=0)
        for w in range(2):
            part = dot(weighted[w], right, ((1,), (1,)))
            for k in range(G):
                acc[k, w * M : (w + 1) * M, :] += part[:, k * L : (k + 1) * L]

    for piece in range(NP):
        chunk, j, nj = PIECES[piece]
        arrive(piece)
        if j == 0:
            keep(chunk).wait()

        def step_gram(jp, carry, chunk=chunk):
            gram(chunk, jp)
            return carry

        last = piece == NP - 1
        lax.fori_loop(j // 2, (j + nj) // 2 - last, step_gram, 0)

    rot, weighted = rotated(NB - 1, B // 2 - 1)
    for k in range(G):
        right_s[k] = jnp.concatenate([rot[k * span : (k + 1) * span], hole], axis=0)
    for w in range(2):
        lhs[w * M : (w + 1) * M] = weighted[w]

    def last_lanes(c):
        right = jnp.concatenate([right_s[2 * s + c] for s in range(2)], axis=0)
        return dot(lhs[...], right, ((1,), (1,)))

    part = last_lanes(1 - core)
    swaps = []
    for s in range(2):
        half_own.at[s].reshape(2 * M, L)[...] = (
            acc[2 * s + 1 - core] + part[:, s * L : (s + 1) * L]
        ).astype(BF16)
        swap = pltpu.make_async_remote_copy(
            src_ref=half_own.at[s],
            dst_ref=half_got.at[s],
            send_sem=c_send.at[s],
            recv_sem=c_recv.at[s],
            device_id=(pair, z * G + xl * 2 + 1 - core),
            device_id_type=MESH,
        )
        swap.start()
        swaps.append(swap)
    part = last_lanes(core)
    for s in range(2):
        acc[2 * s + core] += part[:, s * L : (s + 1) * L]
    for s in range(2):
        swaps[s].wait_recv()
        both = acc[2 * s + core] + half_got.at[s].reshape(2 * M, L)[...].astype(F32)
        plane_src.at[s].reshape(2 * M, L)[...] = both.astype(BF16)

    hops = []
    for d in range(1, PLANE + 1):
        yy, hh, ll = plane_peer(d)
        hop = pltpu.make_async_remote_copy(
            src_ref=plane_src.at[ll, :, :, yy * 2 + hh],
            dst_ref=plane_got.at[d],
            send_sem=p_send.at[d - 1],
            recv_sem=p_recv.at[d - 1],
            device_id=(yy * 2 + hh, z * G + ll * 2 + core),
            device_id_type=MESH,
        )
        hop.start()
        hops.append(hop)
    wide_rows = 2 * M // PAIRS
    kept = pltpu.make_async_copy(plane_src.at[xl, :, :, pair], plane_got.at[0], local.at[NB])
    kept.start()
    kept.wait()
    whole = plane_got.at[0].reshape(wide_rows, L)[...].astype(F32)
    for d in range(1, PLANE + 1):
        hops[d - 1].wait_recv()
        whole = whole + plane_got.at[d].reshape(wide_rows, L)[...].astype(F32)

    square = jnp.concatenate([whole, jnp.zeros((L - wide_rows, L), F32)], axis=0)
    turned.reshape(L, L)[...] = square.T
    rises = []
    for d in range(1, Z):
        zz = lax.rem(z + d, Z)
        rise = pltpu.make_async_remote_copy(
            src_ref=turned.at[pl.ds(3 * zz, 3)],
            dst_ref=z_got.at[d],
            send_sem=z_send.at[d - 1],
            recv_sem=z_recv.at[d - 1],
            device_id=(pair, zz * G + g),
            device_id_type=MESH,
        )
        rise.start()
        rises.append(rise)
    stay = pltpu.make_async_copy(turned.at[pl.ds(3 * z, 3)], z_got.at[0], local.at[NB + 1])
    stay.start()
    stay.wait()
    result = z_got.at[0].reshape(B, L)[...]
    for d in range(1, Z):
        rises[d - 1].wait_recv()
        result = result + z_got.at[d].reshape(B, L)[...]

    cols = M // PAIRS
    row_id = mode * B + lax.broadcasted_iota(jnp.int32, (B, cols), 0)
    col_id = pair * cols + lax.broadcasted_iota(jnp.int32, (B, cols), 1)
    scale = 1.0 / (M * math.sqrt(PAIRS))
    for w in range(2):
        out[:, w, :] = jnp.where(row_id == col_id, 0.0, result[:, w * cols : (w + 1) * cols] * scale)

    def sent(i, carry):
        for piece in range(NP):
            ship(piece, i, z, mate(1)).wait_send()
        return carry

    lax.fori_loop(0, PEERS, sent, 0)
    for copy in swaps + hops + rises:
        copy.wait_send()


def shards(phi, eigvecs, freqs, occupations, smearing, probes, pair_index):
    k = np.arange(M)
    natural = (k % (M // G)) // B * (G * B) + k // (M // G) * B + k % B
    perm = jnp.asarray(np.equal(natural[:, None], k[None, :]), BF16)
    vmem = pl.BlockSpec(memory_space=pltpu.VMEM)
    hbm = pl.BlockSpec(memory_space=pl.ANY)
    smem = pl.BlockSpec(memory_space=pltpu.SMEM)
    dma = pltpu.SemaphoreType.DMA
    return pl.pallas_call(
        kernel,
        out_shape=jax.ShapeDtypeStruct((B, 2, M // PAIRS), F32),
        in_specs=[smem, smem, hbm, hbm] + [vmem] * 4,
        out_specs=vmem,
        scratch_shapes=[
            pltpu.VMEM((B, M, M), BF16),
            pltpu.VMEM(eigvecs.shape, BF16),
            pltpu.VMEM((2 * M, 2 * L), BF16),
            pltpu.VMEM((G, L, 2 * L), BF16),
            pltpu.VMEM((M, M), BF16),
            pltpu.VMEM((M, M), BF16),
            pltpu.VMEM((M, M), BF16),
            pltpu.VMEM((NB, M * B, L), F32),
            pltpu.VMEM((M * B, M), BF16),
            pltpu.VMEM((NB, Z * G, B, 3, 4, L), BF16),
            pltpu.VMEM((NB, B, M // 4, 4, L), BF16),
            pltpu.VMEM((2, B, 1, M), F32),
            pltpu.VMEM((G, 2 * M, L), F32),
            pltpu.VMEM((2, 2 * M // 4, 4, L), BF16),
            pltpu.VMEM((2, 2 * M // 4, 4, L), BF16),
            pltpu.VMEM((2, 2, G, Z, 3, 4, L), BF16),
            pltpu.VMEM((PLANE + 1, 2, G, 3, 4, L), BF16),
            pltpu.VMEM((L // 4, 4, L), F32),
            pltpu.VMEM((Z, 3, 4, L), F32),
            dma((NP, PEERS)),
            dma((NP, PEERS)),
            dma((2,)),
            dma((2,)),
            dma((PLANE,)),
            dma((PLANE,)),
            dma((Z - 1,)),
            dma((Z - 1,)),
            dma((NB + 2,)),
            dma((B // 2 + 1,)),
        ],
        compiler_params=pltpu.CompilerParams(
            collective_id=0, has_side_effects=True, vmem_limit_bytes=60 * 1024 * 1024
        ),
        name="sigma",
    )(pair_index, probes, phi, eigvecs, freqs, occupations, smearing, perm)


def solution(mesh):
    return jax.shard_map(
        shards,
        mesh=mesh,
        in_specs=(
            P("pair", "mode", None, None),
            P(),
            P(),
            P(),
            P(),
            P("pair", None),
            P("pair", None),
        ),
        out_specs=P("mode", None, "pair"),
        check_vma=False,
    )
```

```python
import math

import jax
import jax.numpy as jnp
from jax import lax
from jax.experimental import pallas as pl
from jax.experimental.pallas import tpu as pltpu
from jax.sharding import PartitionSpec as P

MESH = pl.DeviceIdType.MESH
F32 = jnp.float32
BF16 = jnp.bfloat16

M = 384
Z = 8
G = 4
L = 128
NB = M // L
B = M // (Z * G)
ROWS = B * B
PEERS = Z * G - 1
PAIRS = 8
PLANE = 15
PIECES = ((0, 0, 12), (1, 0, 12), (2, 0, 6), (2, 6, 4), (2, 10, 2))
NP = len(PIECES)


def lorentz(offset, eta):
    return eta / (offset * offset + eta * eta)


def dot(a, b, dims=((1,), (0,))):
    return lax.dot_general(a, b, (dims, ((), ())), preferred_element_type=F32)


def kernel(
    pidx, probes, phi_hbm, eig_hbm, freqs_hbm, occ_hbm, smear_hbm, out,
    phi, eig, freqs, occ, smear, u_part, send_first, lhs, right_s, e_two_t, e_one, e_three_t, u_f, send, recv, wgt, acc, half_own, half_got, plane_src,
    plane_got, turned, z_got,
    a_send, a_recv, c_send, c_recv, p_send, p_recv, z_send, z_recv, local, loads,
):
    mode = lax.axis_index("mode")
    pair = lax.axis_index("pair")
    z = mode // G
    g = lax.rem(mode, G)
    xl = g // 2
    core = lax.rem(g, 2)
    y = pair // 2
    xh = lax.rem(pair, 2)

    def mate(e):
        return lax.rem(xl + e // 2, 2) * 2 + lax.rem(core + e % 2, 2)

    def plane_peer(d):
        return lax.rem(y + d // 4, 4), lax.rem(xh + (d // 2) % 2, 2), lax.rem(xl + d % 2, 2)

    def plane_back(d):
        return lax.rem(y + 4 - d // 4, 4), lax.rem(xh + (d // 2) % 2, 2), lax.rem(xl + d % 2, 2)

    load_eig = pltpu.make_async_copy(eig_hbm, eig, loads.at[B // 2])
    load_eig.start()

    def load_phi(n):
        two = pl.ds(2 * n, 2)
        return pltpu.make_async_copy(phi_hbm.at[0, two], phi.at[two], loads.at[n])

    for n in range(B // 2):
        load_phi(n).start()
    tables = [
        pltpu.make_async_copy(source, table, loads.at[B // 2 + 1 + n])
        for n, (source, table) in enumerate(
            ((freqs_hbm, freqs), (occ_hbm, occ), (smear_hbm, smear))
        )
    ]
    for table in tables:
        table.start()

    barrier = pltpu.get_barrier_semaphore()

    def greet(i, carry):
        other = lax.rem(mode + 1 + i, Z * G)
        pl.semaphore_signal(barrier, inc=1, device_id=(pair, other), device_id_type=MESH)
        return carry

    lax.fori_loop(0, PEERS, greet, 0)
    for d in range(2, PLANE + 1):
        yy, hh, ll = plane_back(d)
        pl.semaphore_signal(
            barrier, inc=1, device_id=(yy * 2 + hh, z * G + ll * 2 + core), device_id_type=MESH
        )

    load_eig.wait()
    q_one = pidx[0, 0]
    q_two = pidx[0, 1]
    q_three = pidx[0, 2]
    rows_i = lax.broadcasted_iota(jnp.int32, (M, M), 0)
    cols_i = lax.broadcasted_iota(jnp.int32, (M, M), 1)
    eye = (rows_i == cols_i).astype(F32).astype(BF16)
    e_two_t[...] = dot(eye, eig[q_two], ((1,), (1,))).astype(BF16)
    e_one[...] = eig[q_one]

    def rotate_two(n, carry):
        load_phi(n).wait()
        rows = dot(e_two_t[...], jnp.concatenate([phi[2 * n], phi[2 * n + 1]], axis=1))
        for c in range(2):
            at = 2 * lax.rem(n, 2) + c
            for b in range(NB):
                value = rows[:, c * M + b * L : c * M + (b + 1) * L]
                u_f[b, pl.ds(2 * n + c, M, stride=B), :] = value
                u_part[b, pl.ds(at, M, stride=4), :] = value
        return carry

    def ship_first(group, zz, gg):
        return pltpu.make_async_remote_copy(
            src_ref=send_first.at[group, zz * G + gg],
            dst_ref=recv.at[0, :, 3 * mode + group],
            send_sem=a_send.at[0],
            recv_sem=a_recv.at[0],
            device_id=(pair, zz * G + gg),
            device_id_type=MESH,
        )

    def keep_first(group):
        return pltpu.make_async_copy(
            send_first.at[group, mode], recv.at[0, :, 3 * mode + group], local.at[group]
        )

    def ship(piece, zz, gg):
        chunk, j, nj = PIECES[piece]
        return pltpu.make_async_remote_copy(
            src_ref=send.at[chunk - 1, zz * G + gg, pl.ds(j, nj)],
            dst_ref=recv.at[chunk, pl.ds(j, nj), pl.ds(3 * mode, 3)],
            send_sem=a_send.at[piece],
            recv_sem=a_recv.at[piece],
            device_id=(pair, zz * G + gg),
            device_id_type=MESH,
        )

    def keep(chunk):
        return pltpu.make_async_copy(
            send.at[chunk - 1, mode], recv.at[chunk, :, pl.ds(3 * mode, 3)], local.at[chunk + 2]
        )

    def everyone(piece):
        chunk, j, nj = PIECES[piece]
        block = recv.at[chunk, pl.ds(j, nj), pl.ds(0, 3 * PEERS)]
        return pltpu.make_async_remote_copy(
            src_ref=block,
            dst_ref=block,
            send_sem=a_send.at[piece],
            recv_sem=a_recv.at[piece],
            device_id=(pair, z * G + mate(1)),
            device_id_type=MESH,
        )

    def far(t):
        h = (t + 1) // 2
        return lax.rem(z + 4 + (1 - 2 * lax.rem(t, 2)) * h, Z)

    def first_group(group, zz):
        size = M * 4 // Z
        start = pl.multiple_of(zz * size, size)
        rows = jnp.concatenate([u_part[b, pl.ds(start, size), :] for b in range(NB)], axis=1)
        done = dot(rows.astype(BF16), e_one[:, :L]).astype(BF16)
        send_first.at[group, pl.ds(zz * G, G)].reshape(size, L)[...] = done

    def later_chunks(zz):
        start = pl.multiple_of(zz * (G * ROWS), G * ROWS)
        rows = jnp.concatenate(
            [u_f[b, pl.ds(start, G * ROWS), :] for b in range(NB)], axis=1
        ).astype(BF16)
        done = dot(rows, e_one[:, L:]).astype(BF16)
        for chunk in range(1, NB):
            send.at[chunk - 1, pl.ds(zz * G, G)].reshape(G * ROWS, L)[...] = done[
                :, (chunk - 1) * L : chunk * L
            ]

    def ship_all(piece, t):
        zz = far(t)
        for e in range(G):
            ship(piece, zz, mate(e)).start()

    def ship_near(piece):
        for e in range(1, G):
            ship(piece, z, mate(e)).start()

    for group in range(3):
        lax.fori_loop(2 * group, 2 * group + 2, rotate_two, 0)
        if group == 0:
            pl.semaphore_wait(barrier, PEERS + PLANE - 1)

        def step_first(t, carry, group=group):
            zz = far(t)
            first_group(group, zz)
            for e in range(G):
                ship_first(group, zz, mate(e)).start()
            return carry

        lax.fori_loop(0, Z - 1, step_first, 0)
        first_group(group, z)
        for e in range(1, G):
            ship_first(group, z, mate(e)).start()
        keep_first(group).start()

    def step_later(t, carry):
        later_chunks(far(t))
        ship_all(1, t)
        return carry

    lax.fori_loop(0, Z - 1, step_later, 0)
    later_chunks(z)
    ship_near(1)
    for chunk in range(1, NB):
        keep(chunk).start()

    for piece in range(2, NP):

        def step_last(t, carry, piece=piece):
            ship_all(piece, t)
            return carry

        lax.fori_loop(0, Z - 1, step_last, 0)
        ship_near(piece)

    row = lax.broadcasted_iota(jnp.int32, (M, 1), 0)
    block = sum((row >= n * (M // G)).astype(jnp.int32) for n in range(1, G))
    within = row - block * (M // G)
    chip = sum((within >= n * B).astype(jnp.int32) for n in range(1, Z))
    natural = within + (G - 1) * B * chip + B * block
    perm = (natural == cols_i).astype(F32).astype(BF16)
    e_three_t[...] = dot(perm, eig[q_three], ((1,), (1,))).astype(BF16)

    for table in tables:
        table.wait()
    lane = lax.broadcasted_iota(jnp.int32, (B, M), 1)
    mine = lane == mode * B + lax.broadcasted_iota(jnp.int32, (B, M), 0)

    def column(table):
        return jnp.sum(jnp.where(mine, table[pl.ds(q_two, 1), :], 0.0), axis=1, keepdims=True)

    f_one = freqs[pl.ds(q_one, 1), :]
    n_one = occ[pl.ds(q_one, 1), :]
    h_one = smear[pl.ds(q_one, 1), :]
    f_two = column(freqs)
    n_two = column(occ)
    h_two = column(smear)
    total = f_two + f_one
    differ = f_two - f_one
    eta = 0.5 * (h_two + h_one)
    bose_sum = 1.0 + n_one + n_two
    bose_diff = n_one - n_two
    for w in range(2):
        omega = probes[0, w]
        value = bose_sum * (lorentz(omega - total, eta) - lorentz(omega + total, eta))
        value = value + bose_diff * (lorentz(omega - differ, eta) - lorentz(omega + differ, eta))
        for j in range(B):
            wgt[w, j] = value[j : j + 1, :]

    acc[...] = jnp.zeros_like(acc)
    span = M // G

    def rotated(chunk, jp):
        block = jnp.concatenate(
            [recv.at[chunk, 2 * jp + s].reshape(M, L)[...] for s in range(2)], axis=1
        )
        rot = dot(e_three_t[...], block).astype(BF16)
        wide = rot.astype(F32)
        weighted = []
        for w in range(2):
            row = jnp.concatenate(
                [wgt[w, 2 * jp + s, :, chunk * L : (chunk + 1) * L] for s in range(2)], axis=1
            )
            weighted.append((wide * row).astype(BF16))
        return rot, weighted

    hole = jnp.zeros((L - span, 2 * L), BF16)

    def gram(chunk, jp):
        rot, weighted = rotated(chunk, jp)
        parts = []
        for k in range(G):
            parts += [rot[k * span : (k + 1) * span], hole]
        right = jnp.concatenate(parts, axis=0)
        for w in range(2):
            part = dot(weighted[w], right, ((1,), (1,)))
            for k in range(G):
                acc[k, w * M : (w + 1) * M, :] += part[:, k * L : (k + 1) * L]

    for piece in range(NP):
        chunk, j, nj = PIECES[piece]
        everyone(piece).wait_recv()
        if chunk == 0:
            for group in range(3):
                keep_first(group).wait()
        elif j == 0:
            keep(chunk).wait()

        def step_gram(jp, carry, chunk=chunk):
            gram(chunk, jp)
            return carry

        last = piece == NP - 1
        lax.fori_loop(j // 2, (j + nj) // 2 - last, step_gram, 0)

    rot, weighted = rotated(NB - 1, B // 2 - 1)
    for k in range(G):
        right_s[k] = jnp.concatenate([rot[k * span : (k + 1) * span], hole], axis=0)
    for w in range(2):
        lhs[w * M : (w + 1) * M] = weighted[w]

    def last_lanes(c):
        right = jnp.concatenate([right_s[2 * s + c] for s in range(2)], axis=0)
        return dot(lhs[...], right, ((1,), (1,)))

    part = last_lanes(1 - core)
    swaps = []
    for s in range(2):
        half_own.at[s].reshape(2 * M, L)[...] = (
            acc[2 * s + 1 - core] + part[:, s * L : (s + 1) * L]
        ).astype(BF16)
        swap = pltpu.make_async_remote_copy(
            src_ref=half_own.at[s],
            dst_ref=half_got.at[s],
            send_sem=c_send.at[s],
            recv_sem=c_recv.at[s],
            device_id=(pair, z * G + xl * 2 + 1 - core),
            device_id_type=MESH,
        )
        swap.start()
        swaps.append(swap)
    part = last_lanes(core)
    for s in range(2):
        acc[2 * s + core] += part[:, s * L : (s + 1) * L]
    for s in range(2):
        swaps[s].wait_recv()
        both = acc[2 * s + core] + half_got.at[s].reshape(2 * M, L)[...].astype(F32)
        plane_src.at[s].reshape(2 * M, L)[...] = both.astype(BF16)

    for d in range(1, PLANE + 1):
        yy, hh, ll = plane_peer(d)
        hop = pltpu.make_async_remote_copy(
            src_ref=plane_src.at[ll, :, :, yy * 2 + hh],
            dst_ref=plane_got.at[d],
            send_sem=p_send,
            recv_sem=p_recv,
            device_id=(yy * 2 + hh, z * G + ll * 2 + core),
            device_id_type=MESH,
        )
        hop.start()
    wide_rows = 2 * M // PAIRS
    kept = pltpu.make_async_copy(plane_src.at[xl, :, :, pair], plane_got.at[0], local.at[6])
    kept.start()
    kept.wait()
    others = plane_got.at[pl.ds(1, PLANE)]
    hops = pltpu.make_async_remote_copy(
        src_ref=others,
        dst_ref=others,
        send_sem=p_send,
        recv_sem=p_recv,
        device_id=(pair, z * G + mate(2)),
        device_id_type=MESH,
    )
    hops.wait_recv()
    whole = plane_got.at[0].reshape(wide_rows, L)[...].astype(F32)
    for d in range(1, PLANE + 1):
        whole = whole + plane_got.at[d].reshape(wide_rows, L)[...].astype(F32)

    square = jnp.concatenate([whole, jnp.zeros((L - wide_rows, L), F32)], axis=0)
    turned.reshape(L, L)[...] = square.T
    for d in range(1, Z):
        zz = lax.rem(z + d, Z)
        rise = pltpu.make_async_remote_copy(
            src_ref=turned.at[pl.ds(3 * zz, 3)],
            dst_ref=z_got.at[d],
            send_sem=z_send,
            recv_sem=z_recv,
            device_id=(pair, zz * G + g),
            device_id_type=MESH,
        )
        rise.start()
    stay = pltpu.make_async_copy(turned.at[pl.ds(3 * z, 3)], z_got.at[0], local.at[7])
    stay.start()
    stay.wait()
    others = z_got.at[pl.ds(1, Z - 1)]
    rises = pltpu.make_async_remote_copy(
        src_ref=others,
        dst_ref=others,
        send_sem=z_send,
        recv_sem=z_recv,
        device_id=(pair, z * G + mate(1)),
        device_id_type=MESH,
    )
    rises.wait_recv()
    result = z_got.at[0].reshape(B, L)[...]
    for d in range(1, Z):
        result = result + z_got.at[d].reshape(B, L)[...]

    cols = M // PAIRS
    row_id = mode * B + lax.broadcasted_iota(jnp.int32, (B, cols), 0)
    col_id = pair * cols + lax.broadcasted_iota(jnp.int32, (B, cols), 1)
    scale = 1.0 / (M * math.sqrt(PAIRS))
    for w in range(2):
        out[:, w, :] = jnp.where(row_id == col_id, 0.0, result[:, w * cols : (w + 1) * cols] * scale)

    for piece in range(NP):
        everyone(piece).wait_send()
    for copy in swaps + [hops, rises]:
        copy.wait_send()


def shards(phi, eigvecs, freqs, occupations, smearing, probes, pair_index):
    vmem = pl.BlockSpec(memory_space=pltpu.VMEM)
    hbm = pl.BlockSpec(memory_space=pl.ANY)
    smem = pl.BlockSpec(memory_space=pltpu.SMEM)
    dma = pltpu.SemaphoreType.DMA
    return pl.pallas_call(
        kernel,
        out_shape=jax.ShapeDtypeStruct((B, 2, M // PAIRS), F32),
        in_specs=[smem, smem] + [hbm] * 5,
        out_specs=vmem,
        scratch_shapes=[
            pltpu.VMEM((B, M, M), BF16),
            pltpu.VMEM(eigvecs.shape, BF16),
            pltpu.VMEM(freqs.shape, F32),
            pltpu.VMEM(freqs.shape, F32),
            pltpu.VMEM(freqs.shape, F32),
            pltpu.VMEM((NB, M * 4, L), F32),
            pltpu.VMEM((3, Z * G, B, 4, L), BF16),
            pltpu.VMEM((2 * M, 2 * L), BF16),
            pltpu.VMEM((G, L, 2 * L), BF16),
            pltpu.VMEM((M, M), BF16),
            pltpu.VMEM((M, M), BF16),
            pltpu.VMEM((M, M), BF16),
            pltpu.VMEM((NB, M * B, L), F32),
            pltpu.VMEM((NB - 1, Z * G, B, 3, 4, L), BF16),
            pltpu.VMEM((NB, B, M // 4, 4, L), BF16),
            pltpu.VMEM((2, B, 1, M), F32),
            pltpu.VMEM((G, 2 * M, L), F32),
            pltpu.VMEM((2, 2 * M // 4, 4, L), BF16),
            pltpu.VMEM((2, 2 * M // 4, 4, L), BF16),
            pltpu.VMEM((2, 2, G, Z, 3, 4, L), BF16),
            pltpu.VMEM((PLANE + 1, 2, G, 3, 4, L), BF16),
            pltpu.VMEM((L // 4, 4, L), F32),
            pltpu.VMEM((Z, 3, 4, L), F32),
            dma((NP,)),
            dma((NP,)),
            dma((2,)),
            dma((2,)),
            dma,
            dma,
            dma,
            dma,
            dma((8,)),
            dma((B // 2 + 4,)),
        ],
        compiler_params=pltpu.CompilerParams(
            collective_id=0, has_side_effects=True, vmem_limit_bytes=60 * 1024 * 1024
        ),
        name="sigma",
    )(pair_index, probes, phi, eigvecs, freqs, occupations, smearing)


def solution(mesh):
    return jax.shard_map(
        shards,
        mesh=mesh,
        in_specs=(
            P("pair", "mode", None, None),
            P(),
            P(),
            P(),
            P(),
            P("pair", None),
            P("pair", None),
        ),
        out_specs=P("mode", None, "pair"),
        check_vma=False,
    )
```

```python
import math

import jax
import jax.numpy as jnp
from jax import lax
from jax.experimental import pallas as pl
from jax.experimental.pallas import tpu as pltpu
from jax.sharding import PartitionSpec as P

MESH = pl.DeviceIdType.MESH
F32 = jnp.float32
BF16 = jnp.bfloat16

M = 384
Z = 8
G = 4
L = 128
NB = M // L
B = M // (Z * G)
ROWS = B * B
PEERS = Z * G - 1
PAIRS = 8
PLANE = 15
PIECES = ((0, 0, 12), (1, 0, 12), (2, 0, 6), (2, 6, 4), (2, 10, 2))
NP = len(PIECES)
HOPS = (10, 9, 11, 6, 14, 8, 5, 7, 13, 15, 2, 4, 12, 1, 3)


def lorentz(offset, eta):
    return eta / (offset * offset + eta * eta)


def dot(a, b, dims=((1,), (0,))):
    return lax.dot_general(a, b, (dims, ((), ())), preferred_element_type=F32)


def kernel(
    pidx_hbm, probes_hbm, phi_hbm, eig_hbm, freqs_hbm, occ_hbm, smear_hbm, out,
    pidx, probes, phi, eig, freqs, occ, smear, u_part, send_first, lhs, right_s, e_two_t, e_one, e_three_t, u_f, send, recv, wgt, acc, half_own, half_got, plane_src,
    plane_got, merged, turned, z_got,
    a_send, a_recv, c_send, c_recv, p_send, p_recv, z_send, z_recv, local, loads,
):
    mode = lax.axis_index("mode")
    pair = lax.axis_index("pair")
    z = mode // G
    g = lax.rem(mode, G)
    xl = g // 2
    core = lax.rem(g, 2)
    y = pair // 2
    xh = lax.rem(pair, 2)

    def mate(e):
        return lax.rem(xl + e // 2, 2) * 2 + lax.rem(core + e % 2, 2)

    def plane_peer(d):
        return lax.rem(y + d // 4, 4), lax.rem(xh + (d // 2) % 2, 2), lax.rem(xl + d % 2, 2)

    def plane_back(d):
        return lax.rem(y + 4 - d // 4, 4), lax.rem(xh + (d // 2) % 2, 2), lax.rem(xl + d % 2, 2)

    def far(t):
        h = (t + 1) // 2
        return lax.rem(z + 4 + (1 - 2 * lax.rem(t, 2)) * h, Z)

    load_index = pltpu.make_async_copy(pidx_hbm, pidx, loads.at[B // 2 + 5])
    load_index.start()
    load_eig = pltpu.make_async_copy(eig_hbm, eig, loads.at[B // 2])
    load_eig.start()

    barrier = pltpu.get_barrier_semaphore()

    def greet(t, carry):
        for gg in range(G):
            pl.semaphore_signal(
                barrier, inc=1, device_id=(pair, far(t) * G + gg), device_id_type=MESH
            )
        return carry

    lax.fori_loop(0, 3, greet, 0)
    for d in HOPS:
        if d >= 2:
            yy, hh, ll = plane_back(d)
            pl.semaphore_signal(
                barrier, inc=1, device_id=(yy * 2 + hh, z * G + ll * 2 + core), device_id_type=MESH
            )
    lax.fori_loop(3, Z - 1, greet, 0)
    for e in range(1, G):
        pl.semaphore_signal(
            barrier, inc=1, device_id=(pair, z * G + mate(e)), device_id_type=MESH
        )

    def load_phi(n):
        two = pl.ds(2 * n, 2)
        return pltpu.make_async_copy(phi_hbm.at[0, two], phi.at[two], loads.at[n])

    for n in range(B // 2):
        load_phi(n).start()
    tables = [
        pltpu.make_async_copy(source, table, loads.at[B // 2 + 1 + n])
        for n, (source, table) in enumerate(
            ((freqs_hbm, freqs), (occ_hbm, occ), (smear_hbm, smear), (probes_hbm, probes))
        )
    ]
    for table in tables:
        table.start()

    load_index.wait()
    load_eig.wait()
    q_one = pidx[0, 0]
    q_two = pidx[0, 1]
    q_three = pidx[0, 2]
    rows_i = lax.broadcasted_iota(jnp.int32, (M, M), 0)
    cols_i = lax.broadcasted_iota(jnp.int32, (M, M), 1)
    eye = (rows_i == cols_i).astype(F32).astype(BF16)
    e_two_t[...] = dot(eye, eig[q_two], ((1,), (1,))).astype(BF16)
    e_one[...] = eig[q_one]

    def rotate_two(n, carry):
        load_phi(n).wait()
        rows = dot(e_two_t[...], jnp.concatenate([phi[2 * n], phi[2 * n + 1]], axis=1))
        for c in range(2):
            at = 2 * lax.rem(n, 2) + c
            for b in range(NB):
                value = rows[:, c * M + b * L : c * M + (b + 1) * L]
                u_f[b, pl.ds(2 * n + c, M, stride=B), :] = value
                u_part[b, pl.ds(at, M, stride=4), :] = value
        return carry

    def ship_first(group, zz, gg):
        return pltpu.make_async_remote_copy(
            src_ref=send_first.at[group, zz * G + gg],
            dst_ref=recv.at[0, :, 3 * mode + group],
            send_sem=a_send.at[0],
            recv_sem=a_recv.at[0],
            device_id=(pair, zz * G + gg),
            device_id_type=MESH,
        )

    def keep_first(group):
        return pltpu.make_async_copy(
            send_first.at[group, mode], recv.at[0, :, 3 * mode + group], local.at[group]
        )

    def ship(piece, zz, gg):
        chunk, j, nj = PIECES[piece]
        return pltpu.make_async_remote_copy(
            src_ref=send.at[chunk - 1, zz * G + gg, pl.ds(j, nj)],
            dst_ref=recv.at[chunk, pl.ds(j, nj), pl.ds(3 * mode, 3)],
            send_sem=a_send.at[piece],
            recv_sem=a_recv.at[piece],
            device_id=(pair, zz * G + gg),
            device_id_type=MESH,
        )

    def keep(chunk):
        return pltpu.make_async_copy(
            send.at[chunk - 1, mode], recv.at[chunk, :, pl.ds(3 * mode, 3)], local.at[chunk + 2]
        )

    def everyone(piece):
        chunk, j, nj = PIECES[piece]
        block = recv.at[chunk, pl.ds(j, nj), pl.ds(0, 3 * PEERS)]
        return pltpu.make_async_remote_copy(
            src_ref=block,
            dst_ref=block,
            send_sem=a_send.at[piece],
            recv_sem=a_recv.at[piece],
            device_id=(pair, z * G + mate(1)),
            device_id_type=MESH,
        )

    def first_group(group, zz):
        size = M * 4 // Z
        start = pl.multiple_of(zz * size, size)
        rows = jnp.concatenate([u_part[b, pl.ds(start, size), :] for b in range(NB)], axis=1)
        done = dot(rows.astype(BF16), e_one[:, :L]).astype(BF16)
        send_first.at[group, pl.ds(zz * G, G)].reshape(size, L)[...] = done

    def later_chunks(zz):
        start = pl.multiple_of(zz * (G * ROWS), G * ROWS)
        rows = jnp.concatenate(
            [u_f[b, pl.ds(start, G * ROWS), :] for b in range(NB)], axis=1
        ).astype(BF16)
        done = dot(rows, e_one[:, L:]).astype(BF16)
        for chunk in range(1, NB):
            send.at[chunk - 1, pl.ds(zz * G, G)].reshape(G * ROWS, L)[...] = done[
                :, (chunk - 1) * L : chunk * L
            ]

    def ship_all(piece, t):
        zz = far(t)
        for e in range(G):
            ship(piece, zz, mate(e)).start()

    def ship_near(piece):
        for e in range(1, G):
            ship(piece, z, mate(e)).start()

    for group in range(3):
        lax.fori_loop(2 * group, 2 * group + 2, rotate_two, 0)
        if group == 0:
            pl.semaphore_wait(barrier, PEERS + PLANE - 1)

        def step_first(t, carry, group=group):
            zz = far(t)
            first_group(group, zz)
            for e in range(G):
                ship_first(group, zz, mate(e)).start()
            return carry

        lax.fori_loop(0, Z - 1, step_first, 0)
        first_group(group, z)
        for e in range(1, G):
            ship_first(group, z, mate(e)).start()
        keep_first(group).start()

    def step_later(t, carry):
        later_chunks(far(t))
        ship_all(1, t)
        return carry

    lax.fori_loop(0, Z - 1, step_later, 0)
    later_chunks(z)
    ship_near(1)
    for chunk in range(1, NB):
        keep(chunk).start()

    for piece in range(2, NP):

        def step_last(t, carry, piece=piece):
            ship_all(piece, t)
            return carry

        lax.fori_loop(0, Z - 1, step_last, 0)
        ship_near(piece)

    row = lax.broadcasted_iota(jnp.int32, (M, 1), 0)
    block = sum((row >= n * (M // G)).astype(jnp.int32) for n in range(1, G))
    within = row - block * (M // G)
    chip = sum((within >= n * B).astype(jnp.int32) for n in range(1, Z))
    natural = within + (G - 1) * B * chip + B * block
    perm = (natural == cols_i).astype(F32).astype(BF16)
    e_three_t[...] = dot(perm, eig[q_three], ((1,), (1,))).astype(BF16)

    for table in tables:
        table.wait()
    lane = lax.broadcasted_iota(jnp.int32, (B, M), 1)
    mine = lane == mode * B + lax.broadcasted_iota(jnp.int32, (B, M), 0)

    def column(table):
        return jnp.sum(jnp.where(mine, table[pl.ds(q_two, 1), :], 0.0), axis=1, keepdims=True)

    f_one = freqs[pl.ds(q_one, 1), :]
    n_one = occ[pl.ds(q_one, 1), :]
    h_one = smear[pl.ds(q_one, 1), :]
    f_two = column(freqs)
    n_two = column(occ)
    h_two = column(smear)
    total = f_two + f_one
    differ = f_two - f_one
    eta = 0.5 * (h_two + h_one)
    bose_sum = 1.0 + n_one + n_two
    bose_diff = n_one - n_two
    for w in range(2):
        omega = probes[0, w]
        value = bose_sum * (lorentz(omega - total, eta) - lorentz(omega + total, eta))
        value = value + bose_diff * (lorentz(omega - differ, eta) - lorentz(omega + differ, eta))
        for j in range(B):
            wgt[w, j] = value[j : j + 1, :]

    acc[...] = jnp.zeros_like(acc)
    span = M // G

    def rotated(chunk, jp):
        block = jnp.concatenate(
            [recv.at[chunk, 2 * jp + s].reshape(M, L)[...] for s in range(2)], axis=1
        )
        rot = dot(e_three_t[...], block).astype(BF16)
        wide = rot.astype(F32)
        weighted = []
        for w in range(2):
            row = jnp.concatenate(
                [wgt[w, 2 * jp + s, :, chunk * L : (chunk + 1) * L] for s in range(2)], axis=1
            )
            weighted.append((wide * row).astype(BF16))
        return rot, weighted

    hole = jnp.zeros((L - span, 2 * L), BF16)

    def gram(chunk, jp):
        rot, weighted = rotated(chunk, jp)
        parts = []
        for k in range(G):
            parts += [rot[k * span : (k + 1) * span], hole]
        right = jnp.concatenate(parts, axis=0)
        for w in range(2):
            part = dot(weighted[w], right, ((1,), (1,)))
            for k in range(G):
                acc[k, w * M : (w + 1) * M, :] += part[:, k * L : (k + 1) * L]

    for piece in range(NP):
        chunk, j, nj = PIECES[piece]
        everyone(piece).wait_recv()
        if chunk == 0:
            for group in range(3):
                keep_first(group).wait()
        elif j == 0:
            keep(chunk).wait()

        def step_gram(jp, carry, chunk=chunk):
            gram(chunk, jp)
            return carry

        last = piece == NP - 1
        lax.fori_loop(j // 2, (j + nj) // 2 - last, step_gram, 0)

    rot, weighted = rotated(NB - 1, B // 2 - 1)
    for k in range(G):
        right_s[k] = jnp.concatenate([rot[k * span : (k + 1) * span], hole], axis=0)
    for w in range(2):
        lhs[w] = weighted[w]

    def last_lanes(c, w):
        right = jnp.concatenate([right_s[2 * s + c] for s in range(2)], axis=0)
        return dot(lhs[w], right, ((1,), (1,)))

    swaps = []
    for w in range(2):
        part = last_lanes(1 - core, w)
        for s in range(2):
            half_own.at[w, s].reshape(M, L)[...] = (
                acc[2 * s + 1 - core, w * M : (w + 1) * M] + part[:, s * L : (s + 1) * L]
            ).astype(BF16)
        swap = pltpu.make_async_remote_copy(
            src_ref=half_own.at[w],
            dst_ref=half_got.at[w],
            send_sem=c_send.at[w],
            recv_sem=c_recv.at[w],
            device_id=(pair, z * G + xl * 2 + 1 - core),
            device_id_type=MESH,
        )
        swap.start()
        swaps.append(swap)
    for w in range(2):
        part = last_lanes(core, w)
        for s in range(2):
            acc[2 * s + core, w * M : (w + 1) * M] += part[:, s * L : (s + 1) * L]

    spare = lax.broadcasted_iota(jnp.int32, (span, L), 1) >= span
    rest = L - span
    kept = []
    for w in range(2):
        swaps[w].wait_recv()
        for s in range(2):
            got = half_got.at[w, s].reshape(M, L)[...].astype(F32)
            both = acc[2 * s + core, w * M : (w + 1) * M] + got
            for n in range(G - 1):
                moved = pltpu.roll(both[(G - 1) * span :], span - rest * n, 1)
                packed = jnp.where(spare, moved, both[n * span : (n + 1) * span])
                plane_src.at[w, s, n].reshape(span, L)[...] = packed.astype(BF16)
        for d in HOPS:
            yy, hh, ll = plane_peer(d)
            pltpu.make_async_remote_copy(
                src_ref=plane_src.at[w, ll, :, yy * 2 + hh],
                dst_ref=plane_got.at[d, w],
                send_sem=p_send,
                recv_sem=p_recv,
                device_id=(yy * 2 + hh, z * G + ll * 2 + core),
                device_id_type=MESH,
            ).start()
        kept.append(
            pltpu.make_async_copy(plane_src.at[w, xl, :, pair], plane_got.at[0, w], local.at[6 + w])
        )
        kept[w].start()
    for w in range(2):
        kept[w].wait()
        merged[w, G - 1] = jnp.zeros((3, 4, L), F32)
    others = plane_got.at[pl.ds(1, PLANE)]
    hops = pltpu.make_async_remote_copy(
        src_ref=others,
        dst_ref=others,
        send_sem=p_send,
        recv_sem=p_recv,
        device_id=(pair, z * G + mate(2)),
        device_id_type=MESH,
    )
    hops.wait_recv()
    some = (G - 1) * B
    for w in range(2):
        whole = plane_got.at[0, w].reshape(some, L)[...].astype(F32)
        for d in range(1, PLANE + 1):
            whole = whole + plane_got.at[d, w].reshape(some, L)[...].astype(F32)
        merged.at[w, pl.ds(0, G - 1)].reshape(some, L)[...] = whole

    wide_rows = 2 * M // PAIRS
    square = jnp.concatenate(
        [merged.reshape(wide_rows, L)[...], jnp.zeros((L - wide_rows, L), F32)], axis=0
    ).T
    col = lax.broadcasted_iota(jnp.int32, (rest, L), 1)
    fourth = ((col >= some) & (col < G * B)) | ((col >= G * B + some) & (col < 2 * G * B))
    for n in range(G - 1):
        moved = pltpu.roll(square[span:], (G - 1 - n) * B, 1)
        rows = square[n * rest : (n + 1) * rest] + jnp.where(fourth, moved, 0.0)
        turned.at[pl.ds(n * rest // 4, rest // 4)].reshape(rest, L)[...] = rows
    for d in (4, 3, 5, 2, 6, 1, 7):
        zz = lax.rem(z + d, Z)
        pltpu.make_async_remote_copy(
            src_ref=turned.at[pl.ds(3 * zz, 3)],
            dst_ref=z_got.at[d],
            send_sem=z_send,
            recv_sem=z_recv,
            device_id=(pair, zz * G + g),
            device_id_type=MESH,
        ).start()
    stay = pltpu.make_async_copy(turned.at[pl.ds(3 * z, 3)], z_got.at[0], local.at[8])
    stay.start()
    stay.wait()
    others = z_got.at[pl.ds(1, Z - 1)]
    rises = pltpu.make_async_remote_copy(
        src_ref=others,
        dst_ref=others,
        send_sem=z_send,
        recv_sem=z_recv,
        device_id=(pair, z * G + mate(1)),
        device_id_type=MESH,
    )
    rises.wait_recv()
    result = z_got.at[0].reshape(B, L)[...]
    for d in range(1, Z):
        result = result + z_got.at[d].reshape(B, L)[...]

    cols = M // PAIRS
    row_id = mode * B + lax.broadcasted_iota(jnp.int32, (B, cols), 0)
    col_id = pair * cols + lax.broadcasted_iota(jnp.int32, (B, cols), 1)
    scale = 1.0 / (M * math.sqrt(PAIRS))
    for w in range(2):
        out[:, w, :] = jnp.where(row_id == col_id, 0.0, result[:, w * cols : (w + 1) * cols] * scale)

    for piece in range(NP):
        everyone(piece).wait_send()
    for copy in swaps + [hops, rises]:
        copy.wait_send()


def shards(phi, eigvecs, freqs, occupations, smearing, probes, pair_index):
    vmem = pl.BlockSpec(memory_space=pltpu.VMEM)
    hbm = pl.BlockSpec(memory_space=pl.ANY)
    dma = pltpu.SemaphoreType.DMA
    return pl.pallas_call(
        kernel,
        out_shape=pltpu.VMEM((B, 2, M // PAIRS), F32),
        in_specs=[hbm] * 7,
        out_specs=vmem,
        scratch_shapes=[
            pltpu.SMEM(pair_index.shape, jnp.int32),
            pltpu.SMEM(probes.shape, F32),
            pltpu.VMEM((B, M, M), BF16),
            pltpu.VMEM(eigvecs.shape, BF16),
            pltpu.VMEM(freqs.shape, F32),
            pltpu.VMEM(freqs.shape, F32),
            pltpu.VMEM(freqs.shape, F32),
            pltpu.VMEM((NB, M * 4, L), F32),
            pltpu.VMEM((3, Z * G, B, 4, L), BF16),
            pltpu.VMEM((2, M, 2 * L), BF16),
            pltpu.VMEM((G, L, 2 * L), BF16),
            pltpu.VMEM((M, M), BF16),
            pltpu.VMEM((M, M), BF16),
            pltpu.VMEM((M, M), BF16),
            pltpu.VMEM((NB, M * B, L), F32),
            pltpu.VMEM((NB - 1, Z * G, B, 3, 4, L), BF16),
            pltpu.VMEM((NB, B, M // 4, 4, L), BF16),
            pltpu.VMEM((2, B, 1, M), F32),
            pltpu.VMEM((G, 2 * M, L), F32),
            pltpu.VMEM((2, 2, M // 4, 4, L), BF16),
            pltpu.VMEM((2, 2, M // 4, 4, L), BF16),
            pltpu.VMEM((2, 2, G - 1, Z, 3, 4, L), BF16),
            pltpu.VMEM((PLANE + 1, 2, G - 1, 3, 4, L), BF16),
            pltpu.VMEM((2, G, 3, 4, L), F32),
            pltpu.VMEM((M // G // 4, 4, L), F32),
            pltpu.VMEM((Z, 3, 4, L), F32),
            dma((NP,)),
            dma((NP,)),
            dma((2,)),
            dma((2,)),
            dma,
            dma,
            dma,
            dma,
            dma((9,)),
            dma((B // 2 + 6,)),
        ],
        compiler_params=pltpu.CompilerParams(
            collective_id=0, has_side_effects=True, vmem_limit_bytes=60 * 1024 * 1024
        ),
        name="sigma",
    )(pair_index, probes, phi, eigvecs, freqs, occupations, smearing)


def solution(mesh):
    return jax.shard_map(
        shards,
        mesh=mesh,
        in_specs=(
            P("pair", "mode", None, None),
            P(),
            P(),
            P(),
            P(),
            P("pair", None),
            P("pair", None),
        ),
        out_specs=P("mode", None, "pair"),
        check_vma=False,
    )
```

```python
import math

import jax
import jax.numpy as jnp
from jax import lax
from jax.experimental import pallas as pl
from jax.experimental.pallas import tpu as pltpu
from jax.sharding import PartitionSpec as P

MESH = pl.DeviceIdType.MESH
F32 = jnp.float32
BF16 = jnp.bfloat16

M = 384
Z = 8
G = 4
L = 128
NB = M // L
B = M // (Z * G)
ROWS = B * B
PEERS = Z * G - 1
PAIRS = 8
PLANE = 15
PIECES = ((0, 0, 12), (1, 0, 12), (2, 0, 6), (2, 6, 4), (2, 10, 2))
NP = len(PIECES)
ORDER = (1, 3, 0, 2)
HOPS = (10, 9, 11, 6, 14, 8, 5, 7, 13, 15, 2, 4, 12, 1, 3)


def lorentz(offset, eta):
    return eta / (offset * offset + eta * eta)


def dot(a, b, dims=((1,), (0,))):
    return lax.dot_general(a, b, (dims, ((), ())), preferred_element_type=F32)


def kernel(
    pidx_hbm, probes_hbm, phi_hbm, eig_hbm, freqs_hbm, occ_hbm, smear_hbm, out,
    pidx, probes, phi, eig, freqs, occ, smear, u_part, send_first, lhs, right_s, e_two_t, e_one, e_three_t, u_f, send, recv, wgt, acc, half_own, half_got, plane_src,
    plane_got, merged, turned, z_got,
    a_send, a_recv, c_send, c_recv, p_send, p_recv, z_send, z_recv, local, loads,
):
    mode = lax.axis_index("mode")
    pair = lax.axis_index("pair")
    z = mode // G
    g = lax.rem(mode, G)
    xl = g // 2
    core = lax.rem(g, 2)
    y = pair // 2
    xh = lax.rem(pair, 2)

    def mate(e):
        return lax.rem(xl + e // 2, 2) * 2 + lax.rem(core + e % 2, 2)

    def plane_peer(d):
        return lax.rem(y + d // 4, 4), lax.rem(xh + (d // 2) % 2, 2), lax.rem(xl + d % 2, 2)

    def plane_back(d):
        return lax.rem(y + 4 - d // 4, 4), lax.rem(xh + (d // 2) % 2, 2), lax.rem(xl + d % 2, 2)

    def far(t):
        h = (t + 1) // 2
        return lax.rem(z + 4 + (1 - 2 * lax.rem(t, 2)) * h, Z)

    load_index = pltpu.make_async_copy(pidx_hbm, pidx, loads.at[B // 2 + 5])
    load_index.start()
    load_eig = pltpu.make_async_copy(eig_hbm, eig, loads.at[B // 2])
    load_eig.start()

    barrier = pltpu.get_barrier_semaphore()

    def greet(t, carry):
        for gg in range(G):
            pl.semaphore_signal(
                barrier, inc=1, device_id=(pair, far(t) * G + gg), device_id_type=MESH
            )
        return carry

    lax.fori_loop(0, 3, greet, 0)
    for d in HOPS:
        if d >= 2:
            yy, hh, ll = plane_back(d)
            pl.semaphore_signal(
                barrier, inc=1, device_id=(yy * 2 + hh, z * G + ll * 2 + core), device_id_type=MESH
            )
    lax.fori_loop(3, Z - 1, greet, 0)
    for e in range(1, G):
        pl.semaphore_signal(
            barrier, inc=1, device_id=(pair, z * G + mate(e)), device_id_type=MESH
        )

    def load_phi(n):
        two = pl.ds(2 * n, 2)
        return pltpu.make_async_copy(phi_hbm.at[0, two], phi.at[two], loads.at[n])

    for n in range(B // 2):
        load_phi(n).start()
    tables = [
        pltpu.make_async_copy(source, table, loads.at[B // 2 + 1 + n])
        for n, (source, table) in enumerate(
            ((freqs_hbm, freqs), (occ_hbm, occ), (smear_hbm, smear), (probes_hbm, probes))
        )
    ]
    for table in tables:
        table.start()

    load_index.wait()
    load_eig.wait()
    q_one = pidx[0, 0]
    q_two = pidx[0, 1]
    q_three = pidx[0, 2]
    rows_i = lax.broadcasted_iota(jnp.int32, (M, M), 0)
    cols_i = lax.broadcasted_iota(jnp.int32, (M, M), 1)
    eye = (rows_i == cols_i).astype(F32).astype(BF16)
    e_two_t[...] = dot(eye, eig[q_two], ((1,), (1,))).astype(BF16)
    e_one[...] = eig[q_one]

    def rotate_two(n, carry):
        load_phi(n).wait()
        rows = dot(e_two_t[...], jnp.concatenate([phi[2 * n], phi[2 * n + 1]], axis=1))
        for c in range(2):
            at = 2 * lax.rem(n, 2) + c
            for b in range(NB):
                value = rows[:, c * M + b * L : c * M + (b + 1) * L]
                u_f[b, pl.ds(2 * n + c, M, stride=B), :] = value
                u_part[b, pl.ds(at, M, stride=4), :] = value
        return carry

    def ship_first(group, zz, gg):
        return pltpu.make_async_remote_copy(
            src_ref=send_first.at[group, zz * G + gg],
            dst_ref=recv.at[0, :, 3 * mode + group],
            send_sem=a_send.at[0],
            recv_sem=a_recv.at[0],
            device_id=(pair, zz * G + gg),
            device_id_type=MESH,
        )

    def keep_first(group):
        return pltpu.make_async_copy(
            send_first.at[group, mode], recv.at[0, :, 3 * mode + group], local.at[group]
        )

    def ship(piece, zz, gg):
        chunk, j, nj = PIECES[piece]
        return pltpu.make_async_remote_copy(
            src_ref=send.at[chunk - 1, zz * G + gg, pl.ds(j, nj)],
            dst_ref=recv.at[chunk, pl.ds(j, nj), pl.ds(3 * mode, 3)],
            send_sem=a_send.at[piece],
            recv_sem=a_recv.at[piece],
            device_id=(pair, zz * G + gg),
            device_id_type=MESH,
        )

    def keep(chunk):
        return pltpu.make_async_copy(
            send.at[chunk - 1, mode], recv.at[chunk, :, pl.ds(3 * mode, 3)], local.at[chunk + 2]
        )

    def everyone(piece):
        chunk, j, nj = PIECES[piece]
        block = recv.at[chunk, pl.ds(j, nj), pl.ds(0, 3 * PEERS)]
        return pltpu.make_async_remote_copy(
            src_ref=block,
            dst_ref=block,
            send_sem=a_send.at[piece],
            recv_sem=a_recv.at[piece],
            device_id=(pair, z * G + mate(1)),
            device_id_type=MESH,
        )

    def first_group(group, zz):
        size = M * 4 // Z
        start = pl.multiple_of(zz * size, size)
        rows = jnp.concatenate([u_part[b, pl.ds(start, size), :] for b in range(NB)], axis=1)
        done = dot(rows.astype(BF16), e_one[:, :L]).astype(BF16)
        send_first.at[group, pl.ds(zz * G, G)].reshape(size, L)[...] = done

    def later_chunks(zz):
        start = pl.multiple_of(zz * (G * ROWS), G * ROWS)
        rows = jnp.concatenate(
            [u_f[b, pl.ds(start, G * ROWS), :] for b in range(NB)], axis=1
        ).astype(BF16)
        done = dot(rows, e_one[:, L:]).astype(BF16)
        for chunk in range(1, NB):
            send.at[chunk - 1, pl.ds(zz * G, G)].reshape(G * ROWS, L)[...] = done[
                :, (chunk - 1) * L : chunk * L
            ]

    def ship_all(piece, t):
        zz = far(t)
        for gg in ORDER:
            ship(piece, zz, gg).start()

    def ship_near(piece):
        for e in range(1, G):
            ship(piece, z, mate(e)).start()

    for group in range(3):
        lax.fori_loop(2 * group, 2 * group + 2, rotate_two, 0)
        if group == 0:
            pl.semaphore_wait(barrier, PEERS + PLANE - 1)

        def step_first(t, carry, group=group):
            zz = far(t)
            first_group(group, zz)
            for gg in ORDER:
                ship_first(group, zz, gg).start()
            return carry

        lax.fori_loop(0, Z - 1, step_first, 0)
        first_group(group, z)
        for e in range(1, G):
            ship_first(group, z, mate(e)).start()
        keep_first(group).start()

    def step_later(t, carry):
        later_chunks(far(t))
        ship_all(1, t)
        return carry

    lax.fori_loop(0, Z - 1, step_later, 0)
    later_chunks(z)
    ship_near(1)
    for chunk in range(1, NB):
        keep(chunk).start()

    for piece in range(2, NP):

        def step_last(t, carry, piece=piece):
            ship_all(piece, t)
            return carry

        lax.fori_loop(0, Z - 1, step_last, 0)
        ship_near(piece)

    row = lax.broadcasted_iota(jnp.int32, (M, 1), 0)
    block = sum((row >= n * (M // G)).astype(jnp.int32) for n in range(1, G))
    within = row - block * (M // G)
    chip = sum((within >= n * B).astype(jnp.int32) for n in range(1, Z))
    natural = within + (G - 1) * B * chip + B * block
    perm = (natural == cols_i).astype(F32).astype(BF16)
    e_three_t[...] = dot(perm, eig[q_three], ((1,), (1,))).astype(BF16)

    for table in tables:
        table.wait()
    lane = lax.broadcasted_iota(jnp.int32, (B, M), 1)
    mine = lane == mode * B + lax.broadcasted_iota(jnp.int32, (B, M), 0)

    def column(table):
        return jnp.sum(jnp.where(mine, table[pl.ds(q_two, 1), :], 0.0), axis=1, keepdims=True)

    f_one = freqs[pl.ds(q_one, 1), :]
    n_one = occ[pl.ds(q_one, 1), :]
    h_one = smear[pl.ds(q_one, 1), :]
    f_two = column(freqs)
    n_two = column(occ)
    h_two = column(smear)
    total = f_two + f_one
    differ = f_two - f_one
    eta = 0.5 * (h_two + h_one)
    bose_sum = 1.0 + n_one + n_two
    bose_diff = n_one - n_two
    for w in range(2):
        omega = probes[0, w]
        value = bose_sum * (lorentz(omega - total, eta) - lorentz(omega + total, eta))
        value = value + bose_diff * (lorentz(omega - differ, eta) - lorentz(omega + differ, eta))
        for j in range(B):
            wgt[w, j] = value[j : j + 1, :]

    acc[...] = jnp.zeros_like(acc)
    span = M // G

    def rotated(chunk, jp):
        block = jnp.concatenate(
            [recv.at[chunk, 2 * jp + s].reshape(M, L)[...] for s in range(2)], axis=1
        )
        rot = dot(e_three_t[...], block).astype(BF16)
        wide = rot.astype(F32)
        weighted = []
        for w in range(2):
            row = jnp.concatenate(
                [wgt[w, 2 * jp + s, :, chunk * L : (chunk + 1) * L] for s in range(2)], axis=1
            )
            weighted.append((wide * row).astype(BF16))
        return rot, weighted

    hole = jnp.zeros((L - span, 2 * L), BF16)

    def gram(chunk, jp):
        rot, weighted = rotated(chunk, jp)
        parts = []
        for k in range(G):
            parts += [rot[k * span : (k + 1) * span], hole]
        right = jnp.concatenate(parts, axis=0)
        for w in range(2):
            part = dot(weighted[w], right, ((1,), (1,)))
            for k in range(G):
                acc[k, w * M : (w + 1) * M, :] += part[:, k * L : (k + 1) * L]

    for piece in range(NP):
        chunk, j, nj = PIECES[piece]
        everyone(piece).wait_recv()
        if chunk == 0:
            for group in range(3):
                keep_first(group).wait()
        elif j == 0:
            keep(chunk).wait()

        def step_gram(jp, carry, chunk=chunk):
            gram(chunk, jp)
            return carry

        last = piece == NP - 1
        lax.fori_loop(j // 2, (j + nj) // 2 - last, step_gram, 0)

    rot, weighted = rotated(NB - 1, B // 2 - 1)
    for k in range(G):
        right_s[k] = jnp.concatenate([rot[k * span : (k + 1) * span], hole], axis=0)
    for w in range(2):
        lhs[w] = weighted[w]

    def last_lanes(c, w):
        right = jnp.concatenate([right_s[2 * s + c] for s in range(2)], axis=0)
        return dot(lhs[w], right, ((1,), (1,)))

    swaps = []
    for w in range(2):
        part = last_lanes(1 - core, w)
        for s in range(2):
            half_own.at[w, s].reshape(M, L)[...] = (
                acc[2 * s + 1 - core, w * M : (w + 1) * M] + part[:, s * L : (s + 1) * L]
            ).astype(BF16)
        swap = pltpu.make_async_remote_copy(
            src_ref=half_own.at[w],
            dst_ref=half_got.at[w],
            send_sem=c_send.at[w],
            recv_sem=c_recv.at[w],
            device_id=(pair, z * G + xl * 2 + 1 - core),
            device_id_type=MESH,
        )
        swap.start()
        swaps.append(swap)
    spare = lax.broadcasted_iota(jnp.int32, (span, L), 1) >= span
    rest = L - span
    kept = []
    for w in range(2):
        part = last_lanes(core, w)
        for s in range(2):
            acc[2 * s + core, w * M : (w + 1) * M] += part[:, s * L : (s + 1) * L]
        swaps[w].wait_recv()
        for s in range(2):
            got = half_got.at[w, s].reshape(M, L)[...].astype(F32)
            both = acc[2 * s + core, w * M : (w + 1) * M] + got
            for n in range(G - 1):
                moved = pltpu.roll(both[(G - 1) * span :], span - rest * n, 1)
                packed = jnp.where(spare, moved, both[n * span : (n + 1) * span])
                plane_src.at[w, s, n].reshape(span, L)[...] = packed.astype(BF16)
        for d in HOPS:
            yy, hh, ll = plane_peer(d)
            pltpu.make_async_remote_copy(
                src_ref=plane_src.at[w, ll, :, yy * 2 + hh],
                dst_ref=plane_got.at[d, w],
                send_sem=p_send,
                recv_sem=p_recv,
                device_id=(yy * 2 + hh, z * G + ll * 2 + core),
                device_id_type=MESH,
            ).start()
        kept.append(
            pltpu.make_async_copy(plane_src.at[w, xl, :, pair], plane_got.at[0, w], local.at[6 + w])
        )
        kept[w].start()
    for w in range(2):
        kept[w].wait()
        merged[w, G - 1] = jnp.zeros((3, 4, L), F32)
    others = plane_got.at[pl.ds(1, PLANE)]
    hops = pltpu.make_async_remote_copy(
        src_ref=others,
        dst_ref=others,
        send_sem=p_send,
        recv_sem=p_recv,
        device_id=(pair, z * G + mate(2)),
        device_id_type=MESH,
    )
    hops.wait_recv()
    some = (G - 1) * B
    for w in range(2):
        whole = plane_got.at[0, w].reshape(some, L)[...].astype(F32)
        for d in range(1, PLANE + 1):
            whole = whole + plane_got.at[d, w].reshape(some, L)[...].astype(F32)
        merged.at[w, pl.ds(0, G - 1)].reshape(some, L)[...] = whole

    wide_rows = 2 * M // PAIRS
    square = jnp.concatenate(
        [merged.reshape(wide_rows, L)[...], jnp.zeros((L - wide_rows, L), F32)], axis=0
    ).T
    col = lax.broadcasted_iota(jnp.int32, (rest, L), 1)
    fourth = ((col >= some) & (col < G * B)) | ((col >= G * B + some) & (col < 2 * G * B))
    for n in range(G - 1):
        moved = pltpu.roll(square[span:], (G - 1 - n) * B, 1)
        rows = square[n * rest : (n + 1) * rest] + jnp.where(fourth, moved, 0.0)
        turned.at[pl.ds(n * rest // 4, rest // 4)].reshape(rest, L)[...] = rows
    for d in (4, 3, 5, 2, 6, 1, 7):
        zz = lax.rem(z + d, Z)
        pltpu.make_async_remote_copy(
            src_ref=turned.at[pl.ds(3 * zz, 3)],
            dst_ref=z_got.at[d],
            send_sem=z_send,
            recv_sem=z_recv,
            device_id=(pair, zz * G + g),
            device_id_type=MESH,
        ).start()
    stay = pltpu.make_async_copy(turned.at[pl.ds(3 * z, 3)], z_got.at[0], local.at[8])
    stay.start()
    stay.wait()
    others = z_got.at[pl.ds(1, Z - 1)]
    rises = pltpu.make_async_remote_copy(
        src_ref=others,
        dst_ref=others,
        send_sem=z_send,
        recv_sem=z_recv,
        device_id=(pair, z * G + mate(1)),
        device_id_type=MESH,
    )
    rises.wait_recv()
    result = z_got.at[0].reshape(B, L)[...]
    for d in range(1, Z):
        result = result + z_got.at[d].reshape(B, L)[...]

    cols = M // PAIRS
    row_id = mode * B + lax.broadcasted_iota(jnp.int32, (B, cols), 0)
    col_id = pair * cols + lax.broadcasted_iota(jnp.int32, (B, cols), 1)
    scale = 1.0 / (M * math.sqrt(PAIRS))
    for w in range(2):
        out[:, w, :] = jnp.where(row_id == col_id, 0.0, result[:, w * cols : (w + 1) * cols] * scale)

    for piece in range(NP):
        everyone(piece).wait_send()
    for copy in swaps + [hops, rises]:
        copy.wait_send()


def shards(phi, eigvecs, freqs, occupations, smearing, probes, pair_index):
    vmem = pl.BlockSpec(memory_space=pltpu.VMEM)
    hbm = pl.BlockSpec(memory_space=pl.ANY)
    dma = pltpu.SemaphoreType.DMA
    return pl.pallas_call(
        kernel,
        out_shape=pltpu.VMEM((B, 2, M // PAIRS), F32),
        in_specs=[hbm] * 7,
        out_specs=vmem,
        scratch_shapes=[
            pltpu.SMEM(pair_index.shape, jnp.int32),
            pltpu.SMEM(probes.shape, F32),
            pltpu.VMEM((B, M, M), BF16),
            pltpu.VMEM(eigvecs.shape, BF16),
            pltpu.VMEM(freqs.shape, F32),
            pltpu.VMEM(freqs.shape, F32),
            pltpu.VMEM(freqs.shape, F32),
            pltpu.VMEM((NB, M * 4, L), F32),
            pltpu.VMEM((3, Z * G, B, 4, L), BF16),
            pltpu.VMEM((2, M, 2 * L), BF16),
            pltpu.VMEM((G, L, 2 * L), BF16),
            pltpu.VMEM((M, M), BF16),
            pltpu.VMEM((M, M), BF16),
            pltpu.VMEM((M, M), BF16),
            pltpu.VMEM((NB, M * B, L), F32),
            pltpu.VMEM((NB - 1, Z * G, B, 3, 4, L), BF16),
            pltpu.VMEM((NB, B, M // 4, 4, L), BF16),
            pltpu.VMEM((2, B, 1, M), F32),
            pltpu.VMEM((G, 2 * M, L), F32),
            pltpu.VMEM((2, 2, M // 4, 4, L), BF16),
            pltpu.VMEM((2, 2, M // 4, 4, L), BF16),
            pltpu.VMEM((2, 2, G - 1, Z, 3, 4, L), BF16),
            pltpu.VMEM((PLANE + 1, 2, G - 1, 3, 4, L), BF16),
            pltpu.VMEM((2, G, 3, 4, L), F32),
            pltpu.VMEM((M // G // 4, 4, L), F32),
            pltpu.VMEM((Z, 3, 4, L), F32),
            dma((NP,)),
            dma((NP,)),
            dma((2,)),
            dma((2,)),
            dma,
            dma,
            dma,
            dma,
            dma((9,)),
            dma((B // 2 + 6,)),
        ],
        compiler_params=pltpu.CompilerParams(
            collective_id=0, has_side_effects=True, vmem_limit_bytes=60 * 1024 * 1024
        ),
        name="sigma",
    )(pair_index, probes, phi, eigvecs, freqs, occupations, smearing)


def solution(mesh):
    return jax.shard_map(
        shards,
        mesh=mesh,
        in_specs=(
            P("pair", "mode", None, None),
            P(),
            P(),
            P(),
            P(),
            P("pair", None),
            P("pair", None),
        ),
        out_specs=P("mode", None, "pair"),
        check_vma=False,
    )
```
